32 devices in a mesh: client: 4 (over z), expert: 4 (over y, x), shard: 2 (over core).
Axes of the slice: x: 2, y: 2, z: 4, core: 2. Of those that a mesh axis runs over, the one named last changes fastest.
Arguments:
- tokens: bfloat16 [4, 512, 2048], P('client', 'expert'), may hold values from -6 to 6
- target: bfloat16 [4, 512, 2048], P('client', 'expert'), may hold values from -6 to 6
- routes: int32 [4, 512, 2], P('client', 'expert'), may hold values from 0 to 7, all different within a row; in each aligned block of 128 rows (0 to 127, 128 to 255, ..., all dimensions but the last counted through in order) at most 32 rows name the same one
- gate_weights: float32 [4, 512, 2], P('client', 'expert'), may hold values from 0.1 to 1
- counts: int32 [4], replicated, may hold values from 128 to 512
- gate_proj: bfloat16 [57344, 2048], P(('expert', 'shard'), 'client'), may hold values from -0.125 to 0.125
- up_proj: bfloat16 [57344, 2048], P(('expert', 'shard'), 'client'), may hold values from -0.125 to 0.125
- down_proj: bfloat16 [57344, 2048], P(('expert', 'shard'), 'client'), may hold values from -0.0625 to 0.0625
- correction: bfloat16 [4, 57344, 2048], P('client', ('expert', 'shard')), may hold values from -6 to 6
Outputs:
- pseudo_gradient: float32 [57344, 2048], P(('expert', 'shard'), 'client')
The draws below stay inside these ranges and needn't reach their ends.
Inputs may be any that keep to these rules, and one draw needn't show every extreme that they name: `routes`: in each aligned block of 128 rows of a client, every expert is named by exactly 32 rows; the 2 ids of a row differ.
All inputs are finite; a program needn't handle non-finite values.
Results may differ from the reference program's by a relative error of at most 0.015.
Values may be sent and summed in bfloat16 or wider, within the bound.
A program may use at most 256 MiB of HBM per device.

```python
import math
import jax
import jax.numpy as jnp
import numpy as np
from jax import lax

D = 2048
FF = 7168
EXPERTS = 8
TOP = 2
LOCAL_STEPS = 2
TOK_DEV = 128
CAP = 32
TOKENS = 512
CLIENTS = 4
UNITS = 7168
N_EXPERT = 4


def touch_ends(values, key, smallest, largest):
    index_at = [jax.random.randint(jax.random.fold_in(key, axis), (), 0, length) for axis, length in enumerate(values.shape)]
    widest = values.shape.index(max(values.shape))
    neighbour = index_at[:widest] + [(index_at[widest] + 1) % values.shape[widest]] + index_at[widest + 1:]
    return values.at[tuple(index_at)].set(smallest).at[tuple(neighbour)].set(largest)


def level_of(rng, dims, cuts, low, high):
    gain = 1.0
    for axis_at, blocks in cuts:
        steps = jax.random.uniform(jax.random.fold_in(jax.random.fold_in(rng, 6), axis_at), (blocks,), jnp.float32, low / len(cuts), high / len(cuts))
        gain = gain * jnp.repeat(jnp.exp(steps), dims[axis_at] // blocks).reshape((-1,) + (1,) * (len(dims) - 1 - axis_at))
    return gain


def shared_out(key, own, number, rows, amount, top, most, lean):
    sequence = jax.random.permutation(key, amount)
    packed, ordinary = load_shares(amount, rows * top, most, lean, True), load_shares(amount, rows * top, most, lean, False)
    places = jnp.arange(amount)

    def named(sizes, offset_by):
        used = int((sizes > 0).sum())
        fixed = max(1, used // 4)
        moved = fixed + (places - fixed + offset_by * (used - fixed)) % max(1, amount - fixed)
        return jnp.zeros((amount,), jnp.int32).at[sequence[jnp.where(places < fixed, places, moved)]].set(jnp.asarray(sizes, jnp.int32))

    sizes = jnp.where(number % 4 == 0, named(packed, number // 4), named(ordinary, number - number // 4 - 1))
    mixed = jax.random.permutation(jax.random.fold_in(own, 3), amount)
    giver, sink = mixed[0:amount // 2 * 2:2], mixed[1:amount // 2 * 2:2]
    room = jnp.minimum(sizes[giver] - 1, most - sizes[sink]) // 2
    room = jnp.where((giver == sequence[0]) | (sink == sequence[0]) | (sizes[sink] == 0), 0, jnp.maximum(room, 0))
    moved = jax.random.randint(jax.random.fold_in(own, 4), (amount // 2,), 0, 1 << 20) % (room + 1)
    sizes = sizes.at[giver].add(-moved).at[sink].add(moved)
    members = jnp.searchsorted(jnp.cumsum(sizes), jnp.arange(rows * top), side="right").astype(jnp.int32)
    table = members.reshape(top, rows).T
    table = table[jax.random.permutation(jax.random.fold_in(own, 1), rows)]
    offset_by = jax.random.randint(jax.random.fold_in(own, 2), (rows, 1), 0, top)
    return jnp.take_along_axis(table, (jnp.arange(top)[None, :] + offset_by) % top, axis=1)


def load_shares(amount, total, most, lean, full):
    weights = [(1 << 20) // math.isqrt(grade ** lean) + 1 for grade in range(1, amount + 1)]
    largest = most if full else min(most, max(-(-total // amount), total * weights[0] // sum(weights)))
    least = 1 if total - largest >= amount - 1 else 0
    given, spare = [largest] + [least] * (amount - 1), total - largest - least * (amount - 1)
    while spare > 0:
        movable = [i for i in range(1, amount) if given[i] < largest] or [i for i in range(1, amount) if given[i] < most]
        pool, left = sum([weights[i] for i in movable]), spare
        for i in movable:
            more = min(most - given[i], max(1, left * weights[i] // pool), spare)
            given[i] = given[i] + more
            spare = spare - more
    return np.array(given)


def gaussian(own_key, extent, deviation, limit, shards=(), kind=jnp.bfloat16):
    factor_of = level_of(own_key, extent, shards, -0.22, 0.18) if shards else 1.0
    drawn = jax.random.normal(own_key, extent, jnp.float32) * deviation * factor_of
    return jnp.minimum(jnp.maximum(drawn, -limit), limit).astype(kind)


def setup_inputs(seed: int = 0) -> dict:
    key_list = jax.random.split(jax.random.key(seed), 10)
    tokens = gaussian(key_list[0], (CLIENTS, TOKENS, D), 1.0, 6.0, ((0, 4), (1, 4)))
    target = gaussian(key_list[1], (CLIENTS, TOKENS, D), 1.0, 6.0, ((0, 4), (1, 4)))
    routes_keys = jax.random.split(jax.random.fold_in(key_list[2], 1), CLIENTS * TOKENS // TOK_DEV)
    routes_turns = jax.random.permutation(jax.random.fold_in(key_list[2], 3), CLIENTS * TOKENS // TOK_DEV)
    routes = jax.vmap(lambda own, number: shared_out(jax.random.fold_in(key_list[2], 2), own, number, TOK_DEV, EXPERTS, TOP, CAP, 2))(routes_keys, routes_turns).reshape((CLIENTS, TOKENS, TOP))
    gate_weights = jnp.clip(0.1 + 0.9 * jax.random.uniform(key_list[3], (CLIENTS, TOKENS, TOP), jnp.float32) ** level_of(key_list[3], (CLIENTS, TOKENS, TOP), ((0, 4), (1, 4)), -0.2, 0.2), 0.1, 1.0)
    counts = touch_ends(jax.random.randint(key_list[4], (CLIENTS,), TOKENS // 4, TOKENS + 1), jax.random.fold_in(key_list[4], 1), TOKENS // 4, TOKENS).astype(jnp.int32)
    gate_proj = gaussian(key_list[5], (EXPERTS * FF, D), D ** -0.5, 0.125, ((0, 8), (1, 4)))
    up_proj = gaussian(key_list[6], (EXPERTS * FF, D), D ** -0.5, 0.125, ((0, 8), (1, 4)))
    down_proj = gaussian(key_list[7], (EXPERTS * FF, D), FF ** -0.5, 0.0625, ((0, 8), (1, 4)))
    correction = gaussian(key_list[8], (CLIENTS, EXPERTS * FF, D), 1.0, 6.0, ((0, 4), (1, 8)))
    return dict(tokens=tokens, target=target, routes=routes, gate_weights=gate_weights, counts=counts, gate_proj=gate_proj, up_proj=up_proj, down_proj=down_proj, correction=correction)


def reference(tokens, target, routes, gate_weights, counts, gate_proj, up_proj, down_proj, correction):
    step_size = 2.0 / FF
    slices = FF // UNITS
    count_total = jnp.sum(counts).astype(jnp.float32)
    contract = (((1,), (1,)), ((), ()))
    result = jnp.zeros((EXPERTS * FF, D), jnp.float32)
    for client in range(CLIENTS):
        features = tokens[client]
        flat_routes = routes[client].reshape(-1)
        gates_flat = gate_weights[client].reshape(-1)
        live_rows = (jnp.arange(TOKENS, dtype=jnp.int32) < counts[client]).astype(jnp.float32)
        goal_rows = target[client].astype(jnp.float32)
        control_shift = correction[client].astype(jnp.float32)
        chosen_list = []
        hidden_list = []
        for expert in range(EXPERTS):
            chosen = jnp.nonzero(flat_routes == expert, size=CAP * N_EXPERT)[0].astype(jnp.int32)
            token_rows = chosen // TOP
            expert_rows = jnp.take(features, token_rows, axis=0)
            gate_block = gate_proj[expert * FF:(expert + 1) * FF]
            up_block = up_proj[expert * FF:(expert + 1) * FF]
            gate_pre = lax.dot_general(expert_rows, gate_block, contract, preferred_element_type=jnp.float32)
            up_pre = lax.dot_general(expert_rows, up_block, contract, preferred_element_type=jnp.float32)
            chosen_list.append(chosen)
            hidden_list.append((jax.nn.silu(gate_pre) * up_pre).astype(jnp.bfloat16))
        iterate = down_proj.astype(jnp.float32)
        grad_sum = jnp.zeros((EXPERTS * FF, D), jnp.float32)
        for step_number in range(LOCAL_STEPS):
            output = jnp.zeros((TOKENS, D), jnp.float32)
            for expert in range(EXPERTS):
                chosen = chosen_list[expert]
                hidden_rows = hidden_list[expert].astype(jnp.float32).reshape(CAP * N_EXPERT, slices, UNITS)
                weight_rows = iterate[expert * FF:(expert + 1) * FF].astype(jnp.bfloat16)
                weight_rows = weight_rows.astype(jnp.float32).reshape(slices, UNITS, D)
                partial_value = jnp.einsum("msu,sud->msd", hidden_rows, weight_rows, precision=lax.Precision.HIGHEST)
                partial_value = lax.optimization_barrier(partial_value.astype(jnp.bfloat16)).astype(jnp.float32)
                row_sum = jnp.sum(partial_value, axis=1)
                weight = jnp.take(gates_flat, chosen, axis=0)
                output = output.at[chosen // TOP].add(weight[:, None] * row_sum)
            residual = live_rows[:, None] * (output - goal_rows)
            gradients = []
            for expert in range(EXPERTS):
                chosen = chosen_list[expert]
                weight = jnp.take(gates_flat, chosen, axis=0)
                cotangent = (weight[:, None] * jnp.take(residual, chosen // TOP, axis=0)).astype(jnp.bfloat16)
                gradients.append(lax.dot_general(hidden_list[expert], cotangent, (((0,), (0,)), ((), ())), preferred_element_type=jnp.float32))
            gradient = jnp.concatenate(gradients, axis=0)
            grad_sum = grad_sum + gradient
            if step_number + 1 < LOCAL_STEPS:
                iterate = iterate - step_size * (gradient + control_shift)
        weight_share = counts[client].astype(jnp.float32) / count_total
        client_term = weight_share * (grad_sum / LOCAL_STEPS + control_shift)
        result = result + lax.optimization_barrier(client_term.astype(jnp.bfloat16)).astype(jnp.float32)
    return result
```

```python
import jax
import jax.numpy as jnp
from jax import lax
from jax.sharding import PartitionSpec as P

FF = 7168
EXPERTS = 8
LOCAL_STEPS = 2


def gather_line(own, count):
    ahead, behind = [own], [own]
    for step in range(1, count):
        up = [(j, j + 1) for j in range(step - 1, count - 1)]
        down = [(j + 1, j) for j in range(0, count - step)]
        behind.append(lax.ppermute(behind[-1], "client", up))
        ahead.append(lax.ppermute(ahead[-1], "client", down))
    return [own] + [ahead[k] + behind[count - k] for k in range(1, count)]


def local(tokens, target, routes, gate_weights, counts, gate_proj, up_proj, down_proj, correction):
    expert_count = lax.axis_size("expert")
    shard_count = lax.axis_size("shard")
    client_count = lax.axis_size("client")
    expert_index = lax.axis_index("expert")
    shard_index = lax.axis_index("shard")
    client_index = lax.axis_index("client")
    unit_count = down_proj.shape[0]
    token_count = tokens.shape[1]
    top_count = routes.shape[2]
    feature_width = tokens.shape[2]
    capacity = token_count * top_count // EXPERTS
    per_index = shard_count * unit_count
    hosted = max(1, per_index // FF)
    copies = max(1, FF // per_index)
    own_expert = (expert_index * shard_count + shard_index) * unit_count // FF
    first_expert = expert_index * per_index // FF
    offset = (own_expert - first_expert) * capacity
    weight_share = counts[client_index].astype(jnp.float32) / jnp.sum(counts).astype(jnp.float32)
    control = correction[0]
    scaled = (weight_share * control.astype(jnp.float32)).astype(jnp.bfloat16)
    control_sum = lax.psum_scatter(scaled, "client", scatter_dimension=1, tiled=True)
    flat_routes = routes[0].reshape(-1)
    onehot = (flat_routes[:, None] == jnp.arange(EXPERTS, dtype=jnp.int32)[None, :]).astype(
        jnp.int32
    )
    rank_of = jnp.sum((jnp.cumsum(onehot, axis=0) - 1) * onehot, axis=1)
    slot_of = flat_routes * capacity + rank_of
    source_of = (
        jnp.zeros((EXPERTS * capacity,), jnp.int32)
        .at[slot_of]
        .set(jnp.arange(token_count * top_count, dtype=jnp.int32))
    )

    def arrange(slots, width):
        blocks = slots.reshape(EXPERTS, capacity, width)
        if copies > 1:
            return jnp.repeat(blocks, copies, axis=0)
        return blocks.reshape(expert_count, hosted * capacity, width)

    def own_of(arrived):
        own_rows = lax.dynamic_slice_in_dim(arrived, offset, capacity, 1)
        return own_rows.reshape(expert_count * capacity, feature_width)

    def send_out(slots):
        blocks = arrange(slots, feature_width)
        arrived = lax.all_to_all(blocks, "expert", split_axis=0, concat_axis=0, tiled=True)
        return own_of(arrived)

    token_slots = jnp.take(tokens[0], source_of // top_count, axis=0)
    features = send_out(token_slots)
    columns = feature_width // client_count
    row_total = features.shape[0]
    pieces = features.reshape(row_total, client_count, columns)
    foreign = lax.all_to_all(pieces, "client", split_axis=1, concat_axis=1, tiled=True)
    gate_parts = jnp.einsum("rcw,uw->cru", foreign, gate_proj, preferred_element_type=jnp.float32)
    up_parts = jnp.einsum("rcw,uw->cru", foreign, up_proj, preferred_element_type=jnp.float32)
    gate_back, up_back = (
        lax.all_to_all(
            gate_parts.astype(jnp.bfloat16), "client", split_axis=0, concat_axis=0, tiled=True
        ).astype(gate_parts.dtype),
        lax.all_to_all(
            up_parts.astype(jnp.bfloat16), "client", split_axis=0, concat_axis=0, tiled=True
        ).astype(up_parts.dtype),
    )
    gate_pre = jnp.sum(gate_back, axis=0)
    up_pre = jnp.sum(up_back, axis=0)
    hidden = (jax.nn.silu(gate_pre) * up_pre).astype(jnp.bfloat16)
    gathered = gather_line(hidden, client_count)
    spread = jnp.concatenate(gathered, axis=0)
    order = (client_index + jnp.arange(client_count, dtype=jnp.int32)) % client_count
    inverse = (jnp.arange(client_count, dtype=jnp.int32) - client_index) % client_count
    by_slot = jnp.dot(spread, down_proj, preferred_element_type=jnp.float32).astype(jnp.bfloat16)
    by_client = jnp.take(by_slot.reshape(client_count, row_total, columns), inverse, axis=0)
    first_piece = lax.all_to_all(by_client, "client", split_axis=0, concat_axis=0, tiled=True)
    first_piece = jnp.swapaxes(first_piece, 0, 1).reshape(row_total, feature_width)
    overlap = lax.dot_general(
        hidden, hidden, (((1,), (1,)), ((), ())), preferred_element_type=jnp.float32
    )
    overlap_high = overlap.astype(jnp.bfloat16)
    overlap_low = (overlap - overlap_high.astype(jnp.float32)).astype(jnp.bfloat16)
    overlap_pair = jnp.concatenate([overlap_high, overlap_low], axis=1)
    shift_piece = jnp.dot(hidden, control, preferred_element_type=jnp.float32)
    gate_rows = gate_weights[0]
    positions = expert_index * token_count + jnp.arange(token_count, dtype=jnp.int32)
    live_rows = (positions < counts[client_index]).astype(jnp.float32)
    sender_expert = (
        (jnp.arange(expert_count, dtype=jnp.int32) * shard_count + shard_index) * unit_count // FF
    )
    flat_gates = gate_rows.reshape(-1)
    sender_slot = sender_expert[:, None] * capacity + jnp.arange(capacity, dtype=jnp.int32)[None, :]
    sender_slot = sender_slot.reshape(-1)
    by_choice = slot_of.reshape(token_count, top_count)
    combine = jnp.sum(
        jnp.where(
            by_choice[:, :, None] == sender_slot[None, None, :], gate_rows[:, :, None], 0.0
        ),
        axis=1,
    )
    combine_high = combine.astype(jnp.bfloat16)
    combine_low = (combine - combine_high.astype(jnp.float32)).astype(jnp.bfloat16)
    combine_pair = jnp.concatenate([combine_high, combine_low], axis=1)
    slot_gates = jnp.take(flat_gates, source_of, axis=0)
    slot_tokens = source_of // top_count
    target_rows = target[0].astype(jnp.float32)
    step_size = 2.0 / FF
    cotangents = []
    for step_number in range(LOCAL_STEPS):
        if step_number == 0:
            partial_value = first_piece
        else:
            moved = sum(cotangents[1:], cotangents[0].astype(jnp.float32))
            moved = moved.astype(jnp.bfloat16)
            drift = jnp.dot(
                overlap_pair,
                jnp.concatenate([moved, moved], axis=0),
                preferred_element_type=jnp.float32,
            )
            partial_value = (
                first_piece.astype(jnp.float32)
                - step_size * (drift + float(step_number) * shift_piece)
            ).astype(jnp.bfloat16)
        returned = lax.all_to_all(
            partial_value.reshape(expert_count, capacity, feature_width),
            "expert",
            split_axis=0,
            concat_axis=0,
            tiled=True,
        ).reshape(expert_count * capacity, feature_width)
        plane_rows = jnp.dot(
            combine_pair,
            jnp.concatenate([returned, returned], axis=0),
            preferred_element_type=jnp.float32,
        ).astype(jnp.bfloat16)
        output = plane_rows.astype(jnp.float32)
        for turn in range(1, shard_count):
            ring = [(j, (j + turn) % shard_count) for j in range(shard_count)]
            output = output + lax.ppermute(plane_rows, "shard", ring).astype(jnp.float32)
        residual = live_rows[:, None] * (output - target_rows)
        cotangent = slot_gates[:, None] * jnp.take(residual, slot_tokens, axis=0)
        cotangents.append(send_out(cotangent.astype(jnp.bfloat16)))
    mean_rows = sum(c.astype(jnp.float32) for c in cotangents)
    mean_rows = (mean_rows * (weight_share / LOCAL_STEPS)).astype(jnp.bfloat16)
    mean_rows = jnp.swapaxes(mean_rows.reshape(row_total, client_count, columns), 0, 1)
    mean_rows = lax.all_to_all(mean_rows, "client", split_axis=0, concat_axis=0, tiled=True)
    mean_rows = jnp.take(mean_rows, order, axis=0).reshape(client_count * row_total, columns)
    gradient = lax.dot_general(
        spread, mean_rows, (((0,), (0,)), ((), ())), preferred_element_type=jnp.float32
    )
    return gradient + control_sum.astype(jnp.float32)


def solution(mesh):
    return jax.shard_map(
        local,
        mesh=mesh,
        in_specs=(
            P("client", "expert", None),
            P("client", "expert", None),
            P("client", "expert", None),
            P("client", "expert", None),
            P(),
            P(("expert", "shard"), "client"),
            P(("expert", "shard"), "client"),
            P(("expert", "shard"), "client"),
            P("client", ("expert", "shard"), None),
        ),
        out_specs=P(("expert", "shard"), "client"),
        check_vma=False,
    )
```

```python
import jax
import jax.numpy as jnp
from jax import lax
from jax.sharding import PartitionSpec as P

FF = 7168
EXPERTS = 8
LOCAL_STEPS = 2


def gather_line(own, count):
    ahead, behind = [own], [own]
    for step in range(1, count):
        up = [(j, j + 1) for j in range(step - 1, count - 1)]
        down = [(j + 1, j) for j in range(0, count - step)]
        behind.append(lax.ppermute(behind[-1], "client", up))
        ahead.append(lax.ppermute(ahead[-1], "client", down))
    arrived = ahead[1][0, 0].astype(jnp.float32) + behind[1][0, 0].astype(jnp.float32)
    blocks = [own] + [ahead[k] + behind[count - k] for k in range(1, count)]
    return blocks, jnp.minimum(jnp.abs(arrived), 0.0)


def local(tokens, target, routes, gate_weights, counts, gate_proj, up_proj, down_proj, correction):
    expert_count = lax.axis_size("expert")
    shard_count = lax.axis_size("shard")
    client_count = lax.axis_size("client")
    expert_index = lax.axis_index("expert")
    shard_index = lax.axis_index("shard")
    client_index = lax.axis_index("client")
    unit_count = down_proj.shape[0]
    token_count = tokens.shape[1]
    top_count = routes.shape[2]
    feature_width = tokens.shape[2]
    capacity = token_count * top_count // EXPERTS
    per_index = shard_count * unit_count
    hosted = max(1, per_index // FF)
    copies = max(1, FF // per_index)
    own_expert = (expert_index * shard_count + shard_index) * unit_count // FF
    first_expert = expert_index * per_index // FF
    offset = (own_expert - first_expert) * capacity
    weight_share = counts[client_index].astype(jnp.float32) / jnp.sum(counts).astype(jnp.float32)
    control = correction[0]
    early_units = unit_count // 2

    def weighted_control(block, share):
        scaled = (share * block.astype(jnp.float32)).astype(jnp.bfloat16)
        first = jnp.minimum(jnp.abs(scaled[0, 0].astype(jnp.float32)), 0.0)
        return lax.psum_scatter(scaled, "client", scatter_dimension=1, tiled=True), first

    early_sum, ready = weighted_control(control[:early_units], weight_share)
    flat_routes = routes[0].reshape(-1)
    onehot = (flat_routes[:, None] == jnp.arange(EXPERTS, dtype=jnp.int32)[None, :]).astype(
        jnp.int32
    )
    rank_of = jnp.sum((jnp.cumsum(onehot, axis=0) - 1) * onehot, axis=1)
    slot_of = flat_routes * capacity + rank_of
    source_of = (
        jnp.zeros((EXPERTS * capacity,), jnp.int32)
        .at[slot_of]
        .set(jnp.arange(token_count * top_count, dtype=jnp.int32))
    )

    def arrange(slots, width):
        blocks = slots.reshape(EXPERTS, capacity, width)
        if copies > 1:
            return jnp.repeat(blocks, copies, axis=0)
        return blocks.reshape(expert_count, hosted * capacity, width)

    def own_of(arrived):
        own_rows = lax.dynamic_slice_in_dim(arrived, offset, capacity, 1)
        return own_rows.reshape(expert_count * capacity, feature_width)

    def send_out(slots):
        blocks = arrange(slots, feature_width)
        arrived = lax.all_to_all(blocks, "expert", split_axis=0, concat_axis=0, tiled=True)
        return own_of(arrived)

    token_slots = jnp.take(tokens[0] + ready.astype(tokens.dtype), source_of // top_count, axis=0)
    features = send_out(token_slots)
    columns = feature_width // client_count
    row_total = features.shape[0]
    pieces = features.reshape(row_total, client_count, columns)
    foreign = lax.all_to_all(pieces, "client", split_axis=1, concat_axis=1, tiled=True)
    gate_parts = jnp.einsum("rcw,uw->cru", foreign, gate_proj, preferred_element_type=jnp.float32)
    up_parts = jnp.einsum("rcw,uw->cru", foreign, up_proj, preferred_element_type=jnp.float32)
    gate_back, up_back = (
        lax.all_to_all(
            gate_parts.astype(jnp.bfloat16), "client", split_axis=0, concat_axis=0, tiled=True
        ).astype(gate_parts.dtype),
        lax.all_to_all(
            up_parts.astype(jnp.bfloat16), "client", split_axis=0, concat_axis=0, tiled=True
        ).astype(up_parts.dtype),
    )
    gate_pre = jnp.sum(gate_back, axis=0)
    up_pre = jnp.sum(up_back, axis=0)
    hidden = (jax.nn.silu(gate_pre) * up_pre).astype(jnp.bfloat16)
    gathered, late = gather_line(hidden, client_count)
    late_sum, _ = weighted_control(control[early_units:], weight_share + late)
    spread = jnp.concatenate(gathered, axis=0)
    order = (client_index + jnp.arange(client_count, dtype=jnp.int32)) % client_count
    inverse = (jnp.arange(client_count, dtype=jnp.int32) - client_index) % client_count
    by_slot = jnp.dot(spread, down_proj, preferred_element_type=jnp.float32).astype(jnp.bfloat16)
    by_client = jnp.take(by_slot.reshape(client_count, row_total, columns), inverse, axis=0)
    first_piece = lax.all_to_all(by_client, "client", split_axis=0, concat_axis=0, tiled=True)
    first_piece = jnp.swapaxes(first_piece, 0, 1).reshape(row_total, feature_width)
    overlap = lax.dot_general(
        hidden, hidden, (((1,), (1,)), ((), ())), preferred_element_type=jnp.float32
    )
    overlap_high = overlap.astype(jnp.bfloat16)
    overlap_low = (overlap - overlap_high.astype(jnp.float32)).astype(jnp.bfloat16)
    overlap_pair = jnp.concatenate([overlap_high, overlap_low], axis=1)
    shift_piece = jnp.dot(hidden, control, preferred_element_type=jnp.float32)
    gate_rows = gate_weights[0]
    positions = expert_index * token_count + jnp.arange(token_count, dtype=jnp.int32)
    live_rows = (positions < counts[client_index]).astype(jnp.float32)
    sender_expert = (
        (jnp.arange(expert_count, dtype=jnp.int32) * shard_count + shard_index) * unit_count // FF
    )
    flat_gates = gate_rows.reshape(-1)
    sender_slot = sender_expert[:, None] * capacity + jnp.arange(capacity, dtype=jnp.int32)[None, :]
    sender_slot = sender_slot.reshape(-1)
    by_choice = slot_of.reshape(token_count, top_count)
    combine = jnp.sum(
        jnp.where(
            by_choice[:, :, None] == sender_slot[None, None, :], gate_rows[:, :, None], 0.0
        ),
        axis=1,
    )
    combine_high = combine.astype(jnp.bfloat16)
    combine_low = (combine - combine_high.astype(jnp.float32)).astype(jnp.bfloat16)
    combine_pair = jnp.concatenate([combine_high, combine_low], axis=1)
    slot_gates = jnp.take(flat_gates, source_of, axis=0)
    slot_tokens = source_of // top_count
    target_rows = target[0].astype(jnp.float32)
    step_size = 2.0 / FF
    cotangents = []
    for step_number in range(LOCAL_STEPS):
        if step_number == 0:
            partial_value = first_piece
        else:
            moved = sum(cotangents[1:], cotangents[0].astype(jnp.float32))
            moved = moved.astype(jnp.bfloat16)
            drift = jnp.dot(
                overlap_pair,
                jnp.concatenate([moved, moved], axis=0),
                preferred_element_type=jnp.float32,
            )
            partial_value = (
                first_piece.astype(jnp.float32)
                - step_size * (drift + float(step_number) * shift_piece)
            ).astype(jnp.bfloat16)
        returned = lax.all_to_all(
            partial_value.reshape(expert_count, capacity, feature_width),
            "expert",
            split_axis=0,
            concat_axis=0,
            tiled=True,
        ).reshape(expert_count * capacity, feature_width)
        plane_rows = jnp.dot(
            combine_pair,
            jnp.concatenate([returned, returned], axis=0),
            preferred_element_type=jnp.float32,
        ).astype(jnp.bfloat16)
        output = plane_rows.astype(jnp.float32)
        for turn in range(1, shard_count):
            ring = [(j, (j + turn) % shard_count) for j in range(shard_count)]
            output = output + lax.ppermute(plane_rows, "shard", ring).astype(jnp.float32)
        residual = live_rows[:, None] * (output - target_rows)
        cotangent = slot_gates[:, None] * jnp.take(residual, slot_tokens, axis=0)
        cotangents.append(send_out(cotangent.astype(jnp.bfloat16)))
    mean_rows = sum(c.astype(jnp.float32) for c in cotangents)
    mean_rows = (mean_rows * (weight_share / LOCAL_STEPS)).astype(jnp.bfloat16)
    mean_rows = jnp.swapaxes(mean_rows.reshape(row_total, client_count, columns), 0, 1)
    mean_rows = lax.all_to_all(mean_rows, "client", split_axis=0, concat_axis=0, tiled=True)
    mean_rows = jnp.take(mean_rows, order, axis=0).reshape(client_count * row_total, columns)
    gradient = lax.dot_general(
        spread, mean_rows, (((0,), (0,)), ((), ())), preferred_element_type=jnp.float32
    )
    control_sum = jnp.concatenate([early_sum, late_sum], axis=0)
    return gradient + control_sum.astype(jnp.float32)


def solution(mesh):
    return jax.shard_map(
        local,
        mesh=mesh,
        in_specs=(
            P("client", "expert", None),
            P("client", "expert", None),
            P("client", "expert", None),
            P("client", "expert", None),
            P(),
            P(("expert", "shard"), "client"),
            P(("expert", "shard"), "client"),
            P(("expert", "shard"), "client"),
            P("client", ("expert", "shard"), None),
        ),
        out_specs=P(("expert", "shard"), "client"),
        check_vma=False,
    )
```
